32 devices in a mesh: dp: 4 (over y, x), ctx: 4 (over z), tensor: 2 (over core).
Axes of the slice: x: 2, y: 2, z: 4, core: 2. Of those that a mesh axis runs over, the one named last changes fastest.
Arguments:
- hidden: bfloat16 [4, 1024, 1024], P('dp', 'ctx'), may hold values from -6 to 6
- segment_ids: int32 [4, 1024], P('dp', 'ctx'), may hold values from 0 to 5, as said below
- cotangent: bfloat16 [4, 1024, 1024], P('dp', 'ctx'), may hold values from -6 to 6
- input_gain: float32 [1024], replicated, may hold values from 0.5 to 1.5
- gate_weight: bfloat16 [1024, 2048], P('dp', 'tensor'), may hold values from -0.1875 to 0.1875
- value_weight: bfloat16 [1024, 2048], P('dp', 'tensor'), may hold values from -0.1875 to 0.1875
- state_weight: bfloat16 [1024, 256], P('dp'), may hold values from -0.1875 to 0.1875
- step_weight: bfloat16 [1024, 32], P('dp', 'tensor'), may hold values from -0.1875 to 0.1875
- conv_weight: float32 [4, 2304], replicated, may hold values from -3 to 3
- conv_bias: float32 [2304], replicated, may hold values from -3 to 3
- step_bias: float32 [32], replicated, may hold values from -4 to -1
- decay_log: float32 [32], replicated, may hold values from -6.5 to -1.5
- skip_gain: float32 [32], replicated, may hold values from 0.5 to 1.5
- mixer_gain: float32 [2048], replicated, may hold values from 0.5 to 1.5
- out_weight: bfloat16 [2048, 1024], P('tensor', 'dp'), may hold values from -0.125 to 0.125
Outputs:
- output: bfloat16 [4, 1024, 1024], P('dp', 'ctx')
- grad_hidden: float32 [4, 1024, 1024], P('dp', 'ctx')
- grad_input_gain: float32 [1024], replicated
- grad_gate_weight: float32 [1024, 2048], P('dp', 'tensor')
- grad_value_weight: float32 [1024, 2048], P('dp', 'tensor')
- grad_state_weight: float32 [1024, 256], P('dp')
- grad_step_weight: float32 [1024, 32], P('dp', 'tensor')
- grad_conv_weight: float32 [4, 2304], replicated
- grad_conv_bias: float32 [2304], replicated
- grad_step_bias: float32 [32], replicated
- grad_decay_log: float32 [32], replicated
- grad_skip_gain: float32 [32], replicated
- grad_mixer_gain: float32 [2048], replicated
- grad_out_weight: float32 [2048, 1024], P('tensor', 'dp')
The draws below stay inside these ranges and needn't reach their ends.
Inputs may be any that keep to these rules, and one draw needn't show every extreme that they name: `segment_ids`: within each sequence the ids start at 0, never fall and rise by one at each new document. Every document has 200 to 512 tokens, except the last one of a sequence, which may be cut short by the sequence's end. The first document of the first sequence has exactly 512 tokens; every document of the last sequence has exactly 200 tokens (the final one possibly cut short).
All inputs are finite; a program needn't handle non-finite values.
Results may differ from the reference program's by a relative error of at most 0.014.
Values may be sent and summed in bfloat16 or wider, within the bound.
A program may use at most 192 MiB of HBM per device.

```python
from functools import partial
import jax
import jax.numpy as jnp
from jax import lax

D = 1024
NH = 32
HD = 64
NS = 128
CW = 4
GROUP = 128
DOC_MIN = 200
DI = 2048
SEQ = 1024
DOC_MAX = 512
SEQS = 4


def draw_segment_ids(key, part):
    count = SEQ // DOC_MIN + 1
    lengths = jax.random.randint(jax.random.fold_in(key, 17), (SEQS, count), DOC_MIN, DOC_MAX + 1)
    lengths = lengths.at[0, 0].set(DOC_MAX)
    lengths = lengths.at[SEQS - 1, :].set(jnp.full((count,), DOC_MIN, jnp.int32))
    ends = jnp.cumsum(lengths, axis=1)
    position = jnp.arange(SEQ, dtype=jnp.int32)
    return jnp.sum((position[None, :, None] >= ends[:, None, :]).astype(jnp.int32), axis=2).astype(jnp.int32)


def block_scale(rng, extent, cuts, low, largest):
    def one(dim, shards_of):
        steps = jax.random.uniform(jax.random.fold_in(jax.random.fold_in(rng, 6), dim), (shards_of,), jnp.float32, low / len(cuts), largest / len(cuts))
        return jnp.repeat(jnp.exp(steps), extent[dim] // shards_of).reshape((-1,) + (1,) * (len(extent) - dim - 1))

    gain = one(*cuts[0])
    for cut in cuts[1:]:
        gain = gain * one(*cut)
    return gain


def scatter_about(own_key, extent, width, bound, cuts=(), kind=jnp.bfloat16):
    array = width * jax.random.normal(own_key, extent, jnp.float32)
    if cuts:
        array = array * block_scale(own_key, extent, cuts, -0.22, 0.18)
    return jnp.clip(array, -bound, bound).astype(kind)


def setup_inputs(seed: int = 0) -> dict:
    arg_keys = jax.random.split(jax.random.key(seed), 16)
    return {
        "hidden": scatter_about(arg_keys[0], (SEQS, SEQ, D), 1.0, 6.0, ((0, 4), (1, 4))),
        "segment_ids": draw_segment_ids(jax.random.fold_in(arg_keys[15], 71), 0),
        "cotangent": scatter_about(arg_keys[2], (SEQS, SEQ, D), 1.0, 6.0, ((0, 4), (1, 4))),
        "input_gain": jnp.clip(1.0 + 0.1 * jax.random.normal(arg_keys[3], (D,), jnp.float32), 0.5, 1.5),
        "gate_weight": scatter_about(arg_keys[4], (D, DI), D ** -0.5, 0.1875, ((0, 4), (1, 2))),
        "value_weight": scatter_about(arg_keys[5], (D, DI), D ** -0.5, 0.1875, ((0, 4), (1, 2))),
        "state_weight": scatter_about(arg_keys[6], (D, 2 * NS), D ** -0.5, 0.1875, ((0, 4),)),
        "step_weight": scatter_about(arg_keys[7], (D, NH), D ** -0.5, 0.1875, ((0, 4), (1, 2))),
        "conv_weight": scatter_about(arg_keys[8], (CW, DI + 2 * NS), CW ** -0.5, 3.0, (), jnp.float32),
        "conv_bias": scatter_about(arg_keys[9], (DI + 2 * NS,), 0.5, 3.0, (), jnp.float32),
        "step_bias": jnp.clip(jax.random.uniform(arg_keys[10], (NH,), jnp.float32, -4.0, -1.0), -4.0, -1.0),
        "decay_log": jnp.clip(jax.random.uniform(arg_keys[11], (NH,), jnp.float32, -6.5, -1.5), -6.5, -1.5),
        "skip_gain": jnp.clip(1.0 + 0.1 * jax.random.normal(arg_keys[12], (NH,), jnp.float32), 0.5, 1.5),
        "mixer_gain": jnp.clip(1.0 + 0.1 * jax.random.normal(arg_keys[13], (DI,), jnp.float32), 0.5, 1.5),
        "out_weight": scatter_about(arg_keys[14], (DI, D), DI ** -0.5, 0.125, ((0, 2), (1, 4))),
    }


epsilon = 1e-05
highest = lax.Precision.HIGHEST

def rms_scale(values, scaling):
    return values * lax.rsqrt(lax.optimization_barrier(jnp.mean(values * values, axis=-1, keepdims=True)) + epsilon) * scaling

def causal_conv(padded, padded_ids, segments, kernel, offset):
    reach = kernel.shape[0] - 1
    length = segments.shape[0]
    total = jnp.broadcast_to(offset[None, :], (length, offset.shape[0]))
    for lag in range(reach + 1):
        begin = reach - lag
        window = padded[begin:begin + length]
        same = (padded_ids[begin:begin + length] == segments).astype(jnp.float32)
        total = total + kernel[lag][None, :] * window * same[:, None]
    return total

def group_step(carry, item, rates):
    values, inputs_b, inputs_c, delta, segments, previous = item
    log_decay = delta * rates[None, :]
    running = jnp.cumsum(log_decay, axis=0)
    length = segments.shape[0]
    order = jnp.arange(length)
    allowed = (segments[:, None] == segments[None, :]) & (order[:, None] >= order[None, :])
    spread = running.T[:, :, None] - running.T[:, None, :]
    decay = jnp.where(allowed[None], jnp.exp(jnp.where(allowed[None], spread, 0.0)), 0.0)
    scores = jnp.dot(inputs_c, inputs_b.T, precision=highest)
    mixing = decay * scores[None] * delta.T[:, None, :]
    inner = jnp.einsum('hts,shp->thp', mixing, values, precision=highest)
    entry = jnp.exp(running) * (segments == previous).astype(jnp.float32)[:, None]
    carried = jnp.einsum('tn,hpn->thp', inputs_c, carry, precision=highest) * entry[:, :, None]
    tail = jnp.exp(running[-1][None, :] - running) * (segments == segments[-1]).astype(jnp.float32)[:, None] * delta
    fade = jnp.exp(running[-1]) * (segments[-1] == previous).astype(jnp.float32)
    update = jnp.einsum('sh,shp,sn->hpn', tail, values, inputs_b, precision=highest)
    return (carry * fade[:, None, None] + update, inner + carried)

def mixer(conv_input, raw_step, gate, kernel, offset, step_bias, decay_log, skip_gain, mixer_gain, segments):
    length = conv_input.shape[0]
    reach = kernel.shape[0] - 1
    padded = jnp.concatenate([jnp.zeros((reach, conv_input.shape[1]), jnp.float32), conv_input], 0)
    padded_ids = jnp.concatenate([jnp.full((reach,), -1, jnp.int32), segments])
    activated = jax.nn.silu(causal_conv(padded, padded_ids, segments, kernel, offset))
    inner_width = NH * HD
    values = activated[:, :inner_width].reshape(length, NH, HD)
    inputs_b = activated[:, inner_width:inner_width + NS]
    inputs_c = activated[:, inner_width + NS:]
    delta = jax.nn.softplus(raw_step + step_bias[None, :])
    rates = -jnp.exp(decay_log)
    count = length // GROUP
    previous = jnp.concatenate([(segments[0] - 1)[None], segments[GROUP - 1::GROUP][:count - 1]]).astype(jnp.int32)
    items = (values.reshape(count, GROUP, NH, HD), inputs_b.reshape(count, GROUP, NS), inputs_c.reshape(count, GROUP, NS), delta.reshape(count, GROUP, NH), segments.reshape(count, GROUP), previous)
    stepper = jax.checkpoint(partial(group_step, rates=rates))
    final, outputs = lax.scan(stepper, jnp.zeros((NH, HD, NS), jnp.float32), items)
    mixed = outputs.reshape(length, NH, HD) + skip_gain[None, :, None] * values
    mixed = mixed.reshape(length, inner_width)
    product = mixed * jax.nn.silu(gate)
    return rms_scale(product, mixer_gain)

def reference(hidden, segment_ids, cotangent, input_gain, gate_weight, value_weight, state_weight, step_weight, conv_weight, conv_bias, step_bias, decay_log, skip_gain, mixer_gain, out_weight):
    inner_width = NH * HD

    def one(totals, item):
        tokens, segments, cotangent_rows = item
        base = tokens.astype(jnp.float32)
        normed_full, norm_back = jax.vjp(rms_scale, base, input_gain)
        normed = normed_full.astype(jnp.bfloat16)
        gate = jnp.dot(normed, gate_weight, preferred_element_type=jnp.float32)
        value_pre = jnp.dot(normed, value_weight, preferred_element_type=jnp.float32).astype(jnp.bfloat16)
        state_pre = jnp.dot(normed, state_weight, preferred_element_type=jnp.float32).astype(jnp.bfloat16)
        raw_step = jnp.dot(normed, step_weight, preferred_element_type=jnp.float32)
        conv_input = jnp.concatenate([value_pre, state_pre], 1).astype(jnp.float32)
        gated_full, mixer_back = jax.vjp(partial(mixer, segments=segments), conv_input, raw_step, gate, conv_weight, conv_bias, step_bias, decay_log, skip_gain, mixer_gain)
        gated = gated_full.astype(jnp.bfloat16)
        result = (base + jnp.dot(gated, out_weight, preferred_element_type=jnp.float32)).astype(jnp.bfloat16)
        grad_gated = jnp.dot(cotangent_rows, out_weight.T, preferred_element_type=jnp.float32)
        grad_out = jnp.dot(gated.T, cotangent_rows, preferred_element_type=jnp.float32)
        grad_input, grad_raw, grad_gate, grad_kernel, grad_offset, grad_bias, grad_decay, grad_skip, grad_mgain = mixer_back(grad_gated)
        low_gate = grad_gate.astype(jnp.bfloat16)
        low_input = grad_input.astype(jnp.bfloat16)
        low_step = grad_raw.astype(jnp.bfloat16)
        grad_normed = jnp.dot(low_gate, gate_weight.T, preferred_element_type=jnp.float32) + jnp.dot(low_input[:, :inner_width], value_weight.T, preferred_element_type=jnp.float32) + jnp.dot(low_input[:, inner_width:], state_weight.T, preferred_element_type=jnp.float32) + jnp.dot(low_step, step_weight.T, preferred_element_type=jnp.float32)
        grad_base, grad_gain = norm_back(grad_normed)
        grad_tokens = cotangent_rows.astype(jnp.float32) + grad_base
        terms = (grad_gain, jnp.dot(normed.T, low_gate, preferred_element_type=jnp.float32), jnp.dot(normed.T, low_input[:, :inner_width], preferred_element_type=jnp.float32), jnp.dot(normed.T, low_input[:, inner_width:], preferred_element_type=jnp.float32), jnp.dot(normed.T, low_step, preferred_element_type=jnp.float32), grad_kernel, grad_offset, grad_bias, grad_decay, grad_skip, grad_mgain, grad_out)
        totals = tuple((left + right for left, right in zip(totals, terms)))
        return (totals, (result, grad_tokens))
    start = (jnp.zeros((D,), jnp.float32), jnp.zeros((D, inner_width), jnp.float32), jnp.zeros((D, inner_width), jnp.float32), jnp.zeros((D, 2 * NS), jnp.float32), jnp.zeros((D, NH), jnp.float32), jnp.zeros((CW, inner_width + 2 * NS), jnp.float32), jnp.zeros((inner_width + 2 * NS,), jnp.float32), jnp.zeros((NH,), jnp.float32), jnp.zeros((NH,), jnp.float32), jnp.zeros((NH,), jnp.float32), jnp.zeros((inner_width,), jnp.float32), jnp.zeros((inner_width, D), jnp.float32))
    totals, (results, grad_rows) = lax.scan(one, start, (hidden, segment_ids, cotangent))
    return (results, grad_rows, totals[0], totals[1], totals[2], totals[3], totals[4], totals[5], totals[6], totals[7], totals[8], totals[9], totals[10], totals[11])
```

```python
from functools import partial

import jax
import jax.numpy as jnp
from jax import lax
from jax.experimental import pallas as pl
from jax.experimental.pallas import tpu as pltpu
from jax.sharding import PartitionSpec as P

epsilon = 1e-05
highest = lax.Precision.HIGHEST
f32, bf16 = jnp.float32, jnp.bfloat16
MESH = pl.DeviceIdType.MESH
VM = pl.BlockSpec(memory_space=pltpu.VMEM)
ANY = pl.BlockSpec(memory_space=pl.ANY)
LIMIT = 56 * 1024 * 1024


def dot(a, b, ca=1, cb=0, precision=None):
    return lax.dot_general(
        a, b, (((ca,), (cb,)), ((), ())), precision=precision, preferred_element_type=f32
    )


def shifted(array, axis, by):
    size = lax.axis_size(axis)
    pairs = [(i, i + by) for i in range(size) if 0 <= i + by < size]
    return lax.ppermute(array, axis, pairs)


def chain_kernel(axis, by, chunks, local_ref, fade_ref, out_ref, landed, outgoing, send, recv):
    size = lax.axis_size(axis)
    me = lax.axis_index(axis)
    follower = lax.rem(me + by + size, size)
    leader = lax.rem(me - by + size, size)
    first, last = (0, size - 1) if by > 0 else (size - 1, 0)
    rows = local_ref.shape[0] // chunks
    barrier = pltpu.get_barrier_semaphore()

    @pl.when(me != first)
    def _():
        pl.semaphore_signal(barrier, inc=1, device_id={axis: leader}, device_id_type=MESH)

    @pl.when(me != last)
    def _():
        pl.semaphore_wait(barrier, 1)

    def copy(c):
        part = pl.ds(c * rows, rows)
        return pltpu.make_async_remote_copy(
            src_ref=outgoing.at[part],
            dst_ref=landed.at[part],
            send_sem=send.at[c],
            recv_sem=recv.at[c],
            device_id={axis: follower},
            device_id_type=MESH,
        )

    @pl.when(me == first)
    def _():
        landed[...] = jnp.zeros_like(landed)

    for c in range(chunks):
        part = pl.ds(c * rows, rows)

        @pl.when(me != first)
        def _():
            copy(c).wait_recv()

        @pl.when(me != last)
        def _():
            total = fade_ref[part, :] * landed[part, :].astype(f32) + local_ref[part, :].astype(f32)
            outgoing[part, :] = total.astype(outgoing.dtype)
            copy(c).start()

    out_ref[...] = landed[...]

    @pl.when(me != last)
    def _():
        for c in range(chunks):
            copy(c).wait_send()


def chain(local, fade, axis, by, ident, chunks=4):
    return pl.pallas_call(
        partial(chain_kernel, axis, by, chunks),
        out_shape=jax.ShapeDtypeStruct(local.shape, local.dtype),
        in_specs=[VM, VM],
        out_specs=VM,
        scratch_shapes=[
            pltpu.VMEM(local.shape, local.dtype),
            pltpu.VMEM(local.shape, local.dtype),
            pltpu.SemaphoreType.DMA((chunks,)),
            pltpu.SemaphoreType.DMA((chunks,)),
        ],
        compiler_params=pltpu.CompilerParams(collective_id=ident, has_side_effects=True),
        name="chain",
    )(local, fade)


def pair_kernel(axis, src_ref, out_ref, slots, send, recv):
    size = lax.axis_size(axis)
    me = lax.axis_index(axis)
    barrier = pltpu.get_barrier_semaphore()
    for k in range(1, size):
        pl.semaphore_signal(
            barrier, inc=1, device_id={axis: lax.rem(me + k, size)}, device_id_type=MESH
        )
    pl.semaphore_wait(barrier, size - 1)
    copies = []
    for k in range(1, size):
        copies.append(
            pltpu.make_async_remote_copy(
                src_ref=src_ref,
                dst_ref=slots.at[k - 1],
                send_sem=send.at[k - 1],
                recv_sem=recv.at[k - 1],
                device_id={axis: lax.rem(me + k, size)},
                device_id_type=MESH,
            )
        )
        copies[-1].start()
    for copy in copies:
        copy.wait()
    total = src_ref[...].astype(f32)
    for k in range(1, size):
        total = total + slots[k - 1].astype(f32)
    out_ref[...] = total


def pair_sum(array, axis, ident):
    size = lax.axis_size(axis)
    return pl.pallas_call(
        partial(pair_kernel, axis),
        out_shape=jax.ShapeDtypeStruct(array.shape, f32),
        in_specs=[VM],
        out_specs=VM,
        scratch_shapes=[
            pltpu.VMEM((size - 1,) + array.shape, array.dtype),
            pltpu.SemaphoreType.DMA((size - 1,)),
            pltpu.SemaphoreType.DMA((size - 1,)),
        ],
        compiler_params=pltpu.CompilerParams(
            collective_id=ident, has_side_effects=True, vmem_limit_bytes=LIMIT
        ),
        name="pair_sum",
    )(array)


def gather_kernel(axis, count, *refs):
    ins, outs = refs[:count], refs[count : 2 * count]
    local, send, recv = refs[2 * count :]
    me = lax.axis_index(axis)
    low, high = lax.rem(me, 2), me // 2
    side = high * 2 + (1 - low)
    other = (1 - high) * 2 + low
    corner = (1 - high) * 2 + (1 - low)
    barrier = pltpu.get_barrier_semaphore()
    for peer in (side, other):
        pl.semaphore_signal(barrier, inc=1, device_id={axis: peer}, device_id_type=MESH)
    own = []
    for a in range(count):
        own.append(pltpu.make_async_copy(ins[a], outs[a].at[me], local.at[a]))
        own[-1].start()
    pl.semaphore_wait(barrier, 2)

    def remote(a, src, dst, slot, peer):
        return pltpu.make_async_remote_copy(
            src_ref=src,
            dst_ref=dst,
            send_sem=send.at[a, slot],
            recv_sem=recv.at[a, slot],
            device_id={axis: peer},
            device_id_type=MESH,
        )

    direct = []
    for a in range(count):
        for slot, peer in ((0, side), (1, other)):
            direct.append(remote(a, ins[a], outs[a].at[me], slot, peer))
            direct[-1].start()
    relays = []
    for a in range(count):
        half = ins[a].shape[0] // 2
        lower, upper = pl.ds(0, half), pl.ds(half, half)
        remote(a, ins[a], outs[a].at[side], 0, side).wait_recv()
        relay = remote(a, outs[a].at[side, lower], outs[a].at[side, lower], 2, other)
        relay.start()
        relays.append(relay)
        remote(a, ins[a], outs[a].at[other], 1, other).wait_recv()
        relay = remote(a, outs[a].at[other, upper], outs[a].at[other, upper], 3, side)
        relay.start()
        relays.append(relay)
    for a in range(count):
        half = ins[a].shape[0] // 2
        lower, upper = pl.ds(0, half), pl.ds(half, half)
        remote(a, outs[a].at[corner, lower], outs[a].at[corner, lower], 2, other).wait_recv()
        remote(a, outs[a].at[corner, upper], outs[a].at[corner, upper], 3, side).wait_recv()
    for copy in direct + relays:
        copy.wait_send()
    for copy in own:
        copy.wait()


def gather(arrays, axis, ident):
    size = lax.axis_size(axis)
    if size != 4:
        return tuple(lax.all_gather(a, axis) for a in arrays)
    count = len(arrays)
    return pl.pallas_call(
        partial(gather_kernel, axis, count),
        out_shape=tuple(jax.ShapeDtypeStruct((size,) + a.shape, a.dtype) for a in arrays),
        in_specs=[VM] * count,
        out_specs=tuple([VM] * count),
        scratch_shapes=[
            pltpu.SemaphoreType.DMA((count,)),
            pltpu.SemaphoreType.DMA((count, 4)),
            pltpu.SemaphoreType.DMA((count, 4)),
        ],
        compiler_params=pltpu.CompilerParams(
            collective_id=ident, has_side_effects=True, vmem_limit_bytes=LIMIT
        ),
        name="gather",
    )(*arrays)


def sigmoid(v):
    return 1.0 / (1.0 + jnp.exp(-v))


def silu(v):
    return v / (1.0 + jnp.exp(-v))


def dsilu(v):
    s = sigmoid(v)
    return s * (1.0 + v * (1.0 - s))


def softplus(v):
    return jnp.maximum(v, 0.0) + jnp.log1p(jnp.exp(-jnp.abs(v)))


def spread_pair(first_lanes, table, pair):
    return jnp.where(first_lanes, table[:, 2 * pair : 2 * pair + 1], table[:, 2 * pair + 1 : 2 * pair + 2])


def lanes_first(length, head):
    return lax.broadcasted_iota(jnp.int32, (length, 2 * head), 1) < head


def negative_mask(segc, segr):
    length = segc.shape[0]
    row = lax.broadcasted_iota(jnp.int32, (length, length), 0)
    col = lax.broadcasted_iota(jnp.int32, (length, length), 1)
    return jnp.where((segc == segr) & (row >= col), 0.0, -1e30).astype(f32)


def tails(run, segc):
    length = segc.shape[0]
    return jnp.exp(run[length - 1 : length, :] - run) * (segc == segc[length - 1 : length]).astype(f32)


def local_kernel(
    width, head, cin, same, taps, offs, raw, bias, rate, segc, segr,
    tot, intra, xs, final, delta_out, run_out, runt_out, wide,
):
    length = segc.shape[0]
    total_width = cin.shape[1]
    states = (total_width - width) // 2
    wide[...] = cin[...].astype(f32)
    lags = taps.shape[0]
    pad = cin.shape[0] - length
    for c in range(total_width // 128):
        part = slice(c * 128, c * 128 + 128)
        acc = jnp.broadcast_to(offs[:, part], (length, 128))
        for j in range(lags):
            acc = acc + taps[j : j + 1, part] * (wide[pad - j : pad - j + length, part] * same[:, j : j + 1])
        tot[:, part] = acc
    delta = softplus(raw[...] + bias[...])
    delta_out[...] = delta
    row = lax.broadcasted_iota(jnp.int32, (length, length), 0)
    col = lax.broadcasted_iota(jnp.int32, (length, length), 1)
    below = (row >= col).astype(f32)
    decay = delta * rate[...]
    run = dot(below, decay, precision=highest)
    run_out[...] = run
    runt = run.T
    runt_out[...] = runt
    b = silu(tot[:, width : width + states]).astype(bf16)
    c = silu(tot[:, width + states :]).astype(bf16)
    scores = dot(c, b, 1, 1)
    negative = negative_mask(segc[...], segr[...])
    first = lanes_first(length, head)
    tail = tails(run, segc[...])
    for pair in range(width // (2 * head)):
        part = slice(pair * 2 * head, (pair + 1) * 2 * head)
        x = (silu(tot[:, part]) * spread_pair(first, delta, pair)).astype(bf16)
        xs[:, part] = x
        x32 = x.astype(f32)
        faded = (x32 * spread_pair(first, tail, pair)).astype(bf16)
        final[part, :] = dot(faded, b, 0, 0).astype(bf16)
        total = None
        for k in range(2):
            h = 2 * pair + k
            w = (jnp.exp(run[:, h : h + 1] - runt[h : h + 1, :] + negative) * scores).astype(bf16)
            xk = jnp.where(first if k == 0 else ~first, x32, 0.0).astype(bf16)
            term = dot(w, xk)
            total = term if total is None else total + term
        intra[:, part] = total


def entries(run, segc, before):
    return jnp.exp(run) * (segc == before).astype(f32)


def product_kernel(
    width, head, inner, ctot_ref, tot, intra, entering, run, segc, before, gate, gg, gain, skip, ysum, sums,
):
    length = segc.shape[0]
    first = lanes_first(length, head)
    c = silu(ctot_ref[...]).astype(bf16)
    entry = entries(run[...], segc[...], before[...])
    squares = jnp.zeros((length, 1), f32)
    project = jnp.zeros((length, 1), f32)
    for pair in range(width // (2 * head)):
        part = slice(pair * 2 * head, (pair + 1) * 2 * head)
        y = intra[:, part] + dot(c, entering[part, :], 1, 1) * spread_pair(first, entry, pair)
        ysum[:, part] = y
        mixed = y + spread_pair(first[:1], skip[...], pair) * silu(tot[:, part])
        product = mixed * silu(gate[:, part])
        squares = squares + jnp.sum(product * product, axis=1, keepdims=True)
        project = project + jnp.sum(gg[:, part] * gain[:, part] * product, axis=1, keepdims=True)
    lane = lax.broadcasted_iota(jnp.int32, sums.shape, 1)
    sums[...] = jnp.where(lane == 0, squares, jnp.where(lane == 1, project, 0.0))


def norm_kernel(
    width, head, inner, ctot_ref, tot, ysum, run, segc, before, gate, gg, gain, skip, sums,
    gated, low_gate, gm, grad_entering, grad_gain,
):
    length = segc.shape[0]
    first = lanes_first(length, head)
    c = silu(ctot_ref[...]).astype(bf16)
    entry = entries(run[...], segc[...], before[...])
    scale = lax.rsqrt(sums[:, 0:1] / inner + epsilon)
    project = scale * sums[:, 1:2] / inner
    for pair in range(width // (2 * head)):
        part = slice(pair * 2 * head, (pair + 1) * 2 * head)
        mixed = ysum[:, part] + spread_pair(first[:1], skip[...], pair) * silu(tot[:, part])
        z = gate[:, part]
        sg = sigmoid(z)
        act = z * sg
        unit = mixed * act * scale
        gated[:, part] = (unit * gain[:, part]).astype(bf16)
        g = gg[:, part]
        grad_gain[:, part] = jnp.sum(g * unit, axis=0, keepdims=True)
        gp = scale * (g * gain[:, part] - unit * project)
        gmix = gp * act
        low_gate[:, part] = (gp * mixed * sg * (1.0 + z * (1.0 - sg))).astype(bf16)
        gmb = gmix.astype(bf16)
        gm[:, part] = gmb
        scaled = (gmb.astype(f32) * spread_pair(first, entry, pair)).astype(bf16)
        grad_entering[part, :] = dot(scaled, c, 0, 0).astype(bf16)


def back_kernel(
    width, head, gm, xs, ysum, tot, cin, same, taps, raw, bias, rate, skip, delta_in, run_in, runt_in,
    segc, segr, before, entering, leaving,
    gpad, gtaps, goffs, graw, gheads, dtot, wide,
):
    length = segc.shape[0]
    heads = width // head
    total_width = tot.shape[1]
    states = (total_width - width) // 2
    first = lanes_first(length, head)
    run, runt, delta = run_in[...], runt_in[...], delta_in[...]
    negative = negative_mask(segc[...], segr[...])
    b = silu(tot[:, width : width + states]).astype(bf16)
    c = silu(tot[:, width + states :]).astype(bf16)
    scores = dot(c, b, 1, 1)
    tail = tails(run, segc[...])
    entry = entries(run, segc[...], before[...])
    dscores = jnp.zeros((length, length), f32)
    u = jnp.zeros((length, heads), f32)
    q = jnp.zeros((1, heads), f32)
    vdx = jnp.zeros((length, heads), f32)
    gv = jnp.zeros((1, heads), f32)
    ge = jnp.zeros((1, heads), f32)
    db = jnp.zeros((length, states), f32)
    dc = jnp.zeros((length, states), f32)
    chan = lax.broadcasted_iota(jnp.int32, (2 * head, heads), 0)
    which = lax.broadcasted_iota(jnp.int32, (2 * head, heads), 1)
    for pair in range(heads // 2):
        part = slice(pair * 2 * head, (pair + 1) * 2 * head)
        pick = (which == 2 * pair + (chan >= head).astype(jnp.int32)).astype(f32)
        x = xs[:, part]
        x32 = x.astype(f32)
        g = gm[:, part]
        g32 = g.astype(f32)
        tl = spread_pair(first, tail, pair)
        grad_f = leaving[part, :]
        late = dot(b, grad_f, 1, 1) * tl
        dx = late
        for k in range(2):
            h = 2 * pair + k
            lanes = first if k == 0 else ~first
            gk = jnp.where(lanes, g32, 0.0).astype(bf16)
            decay = jnp.exp(run[:, h : h + 1] - runt[h : h + 1, :] + negative)
            w = (decay * scores).astype(bf16)
            dscores = dscores + decay * dot(gk, x, 1, 1)
            dx = dx + dot(w, gk, 0, 0)
        raw_v = tot[:, part]
        sg = sigmoid(raw_v)
        v = raw_v * sg
        u = u + dot(g32 * ysum[:, part] - x32 * dx, pick, precision=highest)
        q = q + jnp.sum(dot(x32 * late, pick, precision=highest), axis=0, keepdims=True)
        vdx = vdx + dot(v * dx, pick, precision=highest)
        gv = gv + dot(jnp.sum(g32 * v, axis=0, keepdims=True), pick, precision=highest)
        per_row = jnp.sum(grad_f.astype(f32) * entering[part, :].astype(f32), axis=1, keepdims=True)
        ge = ge + jnp.sum(per_row * pick, axis=0, keepdims=True)
        dv = spread_pair(first, delta, pair) * dx + spread_pair(first[:1], skip[...], pair) * g32
        dtot[:, part] = dv * (sg * (1.0 + raw_v * (1.0 - sg)))
        db = db + dot((x32 * tl).astype(bf16), grad_f)
        dc = dc + dot((g32 * spread_pair(first, entry, pair)).astype(bf16), entering[part, :])
    dsb = dscores.astype(bf16)
    dc = dc + dot(dsb, b)
    db = db + dot(dsb, c, 0, 0)
    dtot[:, width : width + states] = db * dsilu(tot[:, width : width + states])
    dtot[:, width + states :] = dc * dsilu(tot[:, width + states :])
    row = lax.broadcasted_iota(jnp.int32, (length, length), 0)
    col = lax.broadcasted_iota(jnp.int32, (length, length), 1)
    above = (row <= col).astype(f32)
    last = slice(length - 1, length)
    dld = dot(above, u, precision=highest) + (q + entry[last, :] * ge)
    ddelta = dld * rate[...] + vdx
    gr = ddelta * sigmoid(raw[...] + bias[...])
    graw[...] = gr
    gheads[...] = jnp.zeros_like(gheads)
    gheads[0:1, :] = jnp.sum(gr, axis=0, keepdims=True)
    gheads[1:2, :] = jnp.sum(dld * delta, axis=0, keepdims=True) * rate[...]
    gheads[2:3, :] = gv
    wide[...] = cin[...].astype(f32)
    gpad[...] = jnp.zeros_like(gpad)
    lags = taps.shape[0]
    pad = cin.shape[0] - length
    for n in range(total_width // 128):
        part = slice(n * 128, n * 128 + 128)
        d = dtot[:, part]
        goffs[:, part] = jnp.sum(d, axis=0, keepdims=True)
        for j in range(lags):
            ds = d * same[:, j : j + 1]
            window = slice(pad - j, pad - j + length)
            gtaps[j : j + 1, part] = jnp.sum(ds * wide[window, part], axis=0, keepdims=True)
            gpad[window, part] = gpad[window, part] + ds * taps[j : j + 1, part]


def call(kernel, outs, args, scratch=(), name=None):
    return pl.pallas_call(
        kernel,
        out_shape=tuple(jax.ShapeDtypeStruct(s, d) for s, d in outs),
        in_specs=[VM] * len(args),
        out_specs=tuple([VM] * len(outs)),
        scratch_shapes=list(scratch),
        compiler_params=pltpu.CompilerParams(vmem_limit_bytes=LIMIT),
        name=name,
    )(*args)


def body(
    hidden,
    segment_ids,
    cotangent,
    input_gain,
    gate_weight,
    value_weight,
    state_weight,
    step_weight,
    conv_weight,
    conv_bias,
    step_bias,
    decay_log,
    skip_gain,
    mixer_gain,
    out_weight,
):
    tokens = hidden[0]
    wrapped = segment_ids[0] % 128
    cot = cotangent[0]
    length, width_in = tokens.shape
    shard = lax.axis_index("tensor")
    shards = lax.axis_size("tensor")
    lags = conv_weight.shape[0]
    reach = lags - 1
    dp = lax.axis_size("dp")
    width = gate_weight.shape[1]
    local_heads = step_weight.shape[1]
    head = width // local_heads
    inner = width * shards
    states = state_weight.shape[1] // 2
    ids_col = jnp.broadcast_to(wrapped[length - reach :].astype(bf16)[:, None], (reach, 128))
    edge = shifted(jnp.concatenate([tokens[length - reach :], ids_col], 1), "ctx", 1)
    narrow = jnp.concatenate(
        [state_weight, step_weight, jnp.zeros((state_weight.shape[0], 128 - local_heads), bf16)], 1
    )
    g_gate, g_value, g_narrow, g_out = gather(
        (gate_weight, value_weight, narrow, out_weight), "dp", 0
    )
    full_gate = g_gate.reshape(width_in, width)
    full_value = g_value.reshape(width_in, width)
    full_narrow = g_narrow.reshape(width_in, narrow.shape[1])
    full_out = jnp.concatenate([g_out[k] for k in range(dp)], 1)
    pad = 8
    base_ext = jnp.concatenate(
        [jnp.zeros((pad - reach, width_in), bf16), edge[:, :width_in], tokens], 0
    ).astype(f32)
    inv_ext = lax.rsqrt(jnp.mean(base_ext * base_ext, axis=-1, keepdims=True) + epsilon)
    normed_ext = (base_ext * inv_ext * input_gain).astype(bf16)
    normed = normed_ext[pad:]
    base = tokens.astype(f32)
    inv = inv_ext[pad:]
    gate = jnp.dot(normed, full_gate, preferred_element_type=f32)
    value_pre = jnp.dot(normed_ext, full_value, preferred_element_type=f32)
    rest_pre = jnp.dot(normed_ext, full_narrow, preferred_element_type=f32)
    cin = jnp.concatenate([value_pre.astype(bf16), rest_pre[:, : 2 * states].astype(bf16)], 1)
    raw_step = rest_pre[pad:, 2 * states : 2 * states + local_heads]
    grad_gated = jnp.dot(cot, full_out.T, preferred_element_type=f32)

    padded_ids = jnp.concatenate([edge[:, width_in].astype(jnp.int32), wrapped])
    before = padded_ids[reach - 1].astype(f32).reshape(1, 1)
    same = jnp.stack(
        [
            (padded_ids[reach - j : reach - j + length] == wrapped).astype(f32)
            for j in range(lags)
        ],
        1,
    )
    segc = wrapped.astype(f32)[:, None]
    segr = wrapped.astype(f32)[None, :]

    def local(array, size):
        return lax.dynamic_slice_in_dim(array, shard * size, size, array.ndim - 1)

    taps = jnp.concatenate([local(conv_weight, width), conv_weight[:, inner:]], 1)
    offs = jnp.concatenate([local(conv_bias, width), conv_bias[inner:]], 0)[None]
    bias = local(step_bias, local_heads)[None]
    rate = -jnp.exp(local(decay_log, local_heads))[None]
    skip = local(skip_gain, local_heads)[None]
    gain = local(mixer_gain, width)[None]
    total_width = width + 2 * states

    tot, intra, xs, final, delta, run, runt = call(
        partial(local_kernel, width, head),
        (
            ((length, total_width), f32),
            ((length, width), f32),
            ((length, width), bf16),
            ((width, states), bf16),
            ((length, local_heads), f32),
            ((length, local_heads), f32),
            ((local_heads, length), f32),
        ),
        (cin, same, taps, offs, raw_step, bias, rate, segc, segr),
        (pltpu.VMEM((length + pad, total_width), f32),),
        "mixer_local",
    )
    through = jnp.exp(run[length - 1]) * (segc[length - 1] == before[0]).astype(f32)
    fade = jnp.broadcast_to(jnp.repeat(through, head)[:, None], (width, 128))
    entering = chain(final, fade, "ctx", 1, 1)
    ctot = tot[:, width + states :]
    ysum, sums = call(
        partial(product_kernel, width, head, inner),
        (((length, width), f32), ((length, 128), f32)),
        (ctot, tot, intra, entering, run, segc, before, gate, grad_gated, gain, skip),
        (),
        "mixer_product",
    )
    sums = pair_sum(sums, "tensor", 2)
    gated, low_gate, gm, grad_entering, grad_mgain = call(
        partial(norm_kernel, width, head, inner),
        (
            ((length, width), bf16),
            ((length, width), bf16),
            ((length, width), bf16),
            ((width, states), bf16),
            ((1, width), f32),
        ),
        (ctot, tot, ysum, run, segc, before, gate, grad_gated, gain, skip, sums),
        (),
        "mixer_norm",
    )
    grad_out = jnp.dot(gated.T, cot, preferred_element_type=f32).astype(bf16)
    grad_gate_w = jnp.dot(normed.T, low_gate, preferred_element_type=f32).astype(bf16)
    out_piece = lax.psum_scatter(grad_out, "dp", scatter_dimension=1, tiled=True)
    gate_piece = lax.psum_scatter(grad_gate_w, "dp", scatter_dimension=0, tiled=True)
    leaving = chain(grad_entering, fade, "ctx", -1, 3)
    gpad, gtaps, goffs, graw, gheads = call(
        partial(back_kernel, width, head),
        (
            ((length + pad, total_width), f32),
            ((lags, total_width), f32),
            ((1, total_width), f32),
            ((length, local_heads), f32),
            ((8, local_heads), f32),
        ),
        (
            gm, xs, ysum, tot, cin, same, taps, raw_step, bias, rate, skip, delta, run, runt,
            segc, segr, before, entering, leaving,
        ),
        (pltpu.VMEM((length, total_width), f32), pltpu.VMEM((length + pad, total_width), f32)),
        "mixer_back",
    )
    edge_grad = shifted(gpad[pad - reach : pad], "ctx", -1)
    grad_input = jnp.concatenate(
        [gpad[pad : pad + length - 8], gpad[pad + length - 8 :] + jnp.pad(edge_grad, ((8 - reach, 0), (0, 0)))], 0
    )
    low_value = grad_input[:, :width].astype(bf16)
    low_rest = jnp.concatenate(
        [
            grad_input[:, width:].astype(bf16),
            graw.astype(bf16),
            jnp.zeros((length, 128 - local_heads), bf16),
        ],
        1,
    )
    low_tail = jnp.concatenate([low_value, low_rest], 1)
    grad_tail_w = jnp.dot(normed.T, low_tail, preferred_element_type=f32).astype(bf16)
    tail_piece = lax.psum_scatter(grad_tail_w, "dp", scatter_dimension=0, tiled=True)
    branch_out = jnp.dot(gated, full_out, preferred_element_type=f32).astype(bf16)
    normed_part = (
        jnp.dot(low_gate, full_gate.T, preferred_element_type=f32)
        + jnp.dot(low_value, full_value.T, preferred_element_type=f32)
        + jnp.dot(low_rest, full_narrow.T, preferred_element_type=f32)
    ).astype(bf16)
    both = pair_sum(jnp.concatenate([branch_out, normed_part], 0), "tensor", 4)
    result = (base + both[:length]).astype(bf16)
    gn = both[length:]
    grad_gain = jnp.sum(gn * base * inv, axis=0)
    gs = gn * input_gain
    grad_base = inv * (gs - base * (inv * inv) * jnp.mean(gs * base, axis=-1, keepdims=True))
    grad_tokens = cot.astype(f32) + grad_base

    out_sum = lax.psum(out_piece, "ctx").astype(f32)
    gate_sum = lax.psum(gate_piece, "ctx").astype(f32)
    tail_sum = lax.psum(tail_piece, "ctx")
    state_sum = pair_sum(tail_sum[:, width : width + 2 * states], "tensor", 5)

    mine = (shard == 0).astype(f32)

    def placed(array, size):
        spots = [jnp.where(shard == k, array, 0.0) for k in range(shards)]
        return jnp.concatenate(spots, -1)

    small = jnp.concatenate(
        [
            (grad_gain * mine)[None],
            jnp.concatenate([placed(gtaps[:, :width], width), gtaps[:, width:]], 1).reshape(1, -1),
            jnp.concatenate([placed(goffs[:, :width], width), goffs[:, width:]], 1),
            placed(grad_mgain, width),
            placed(gheads[0:1], local_heads),
            placed(gheads[1:2], local_heads),
            placed(gheads[2:3], local_heads),
        ],
        1,
    )
    sizes = [width_in, lags * (inner + 2 * states), inner + 2 * states, inner]
    sizes = sizes + [local_heads * shards] * 3
    totals = lax.psum(small, ("dp", "ctx", "tensor"))[0]
    parts, at = [], 0
    for size in sizes:
        parts.append(totals[at : at + size])
        at += size
    return (
        result[None],
        grad_tokens[None],
        parts[0],
        gate_sum,
        tail_sum[:, :width].astype(f32),
        state_sum,
        tail_sum[:, width + 2 * states : width + 2 * states + local_heads].astype(f32),
        parts[1].reshape(lags, inner + 2 * states),
        parts[2],
        parts[4],
        parts[5],
        parts[6],
        parts[3],
        out_sum,
    )


def solution(mesh):
    in_specs = (
        P("dp", "ctx", None),
        P("dp", "ctx"),
        P("dp", "ctx", None),
        P(),
        P("dp", "tensor"),
        P("dp", "tensor"),
        P("dp", None),
        P("dp", "tensor"),
        P(),
        P(),
        P(),
        P(),
        P(),
        P(),
        P("tensor", "dp"),
    )
    out_specs = (
        P("dp", "ctx", None),
        P("dp", "ctx", None),
        P(),
        P("dp", "tensor"),
        P("dp", "tensor"),
        P("dp", None),
        P("dp", "tensor"),
        P(),
        P(),
        P(),
        P(),
        P(),
        P(),
        P("tensor", "dp"),
    )
    return jax.shard_map(body, mesh=mesh, in_specs=in_specs, out_specs=out_specs, check_vma=False)
```
